256 devices in a mesh: dp: 32 (over y, x, core), shard: 8 (over z).
Axes of the slice: x: 4, y: 4, z: 8, core: 2. Of those that a mesh axis runs over, the one named last changes fastest.
Arguments:
- grads: bfloat16 [2, 32, 4096, 4096], P(None, 'dp', 'shard'), may hold values from -0.5 to 0.5
- basis: float32 [2, 4096, 256], P(None, 'shard'), may hold values from -0.375 to 0.375
- weight: float32 [2, 8, 32, 16, 4096], P(None, 'shard', 'dp'), may hold values from -6 to 6
- moment_m: float32 [2, 4096, 256], P(None, 'dp'), may hold values from -6 to 6
- moment_v: float32 [2, 4096, 256], P(None, 'dp'), may hold values from 0.25 to 4
Outputs:
- new_weight: float32 [2, 8, 32, 16, 4096], P(None, 'shard', 'dp')
- new_m: float32 [2, 4096, 256], P(None, 'dp')
- new_v: float32 [2, 4096, 256], P(None, 'dp')
- new_basis: float32 [2, 4096, 256], P(None, 'shard')
The draws below stay inside these ranges and needn't reach their ends.
All inputs are finite; a program needn't handle non-finite values.
Results may differ from the reference program's by a relative error of at most 0.0036.
Values may be sent and summed in bfloat16 or wider, within the bound.
A program may use at most 64 MiB of HBM per device.

```python
import math
import jax
import jax.numpy as jnp
from jax import lax

D = 4096
RANK = 256
MATS = 2
NS_STEPS = 5
GROUPS = 32
ROWW = 16
N_DP = 32
N_SHARD = 8


def strengthened(array, rng, source, target, shards_of, factor):
    owner, partner = [(jnp.arange(array.shape[dim]) // (array.shape[dim] // shards_of)).reshape([-1 if axis == dim else 1 for axis in range(array.ndim)]) for dim in (source, target)]
    chosen = jax.random.permutation(rng, shards_of)[partner]
    strong = (owner == chosen) | (owner == (partner + shards_of // 2) % shards_of)
    return jnp.where(strong, factor * array, array)


def level_of(stream_key, dims, shards, low, high):
    factor_of = 1.0
    for position, parts in shards:
        steps = jax.random.uniform(jax.random.fold_in(jax.random.fold_in(stream_key, 6), position), (parts,), jnp.float32, low / len(shards), high / len(shards))
        factor_of = factor_of * jnp.repeat(jnp.exp(steps), dims[position] // parts).reshape((-1,) + (1,) * (len(dims) - 1 - position))
    return factor_of


def centred(key, shape, scale, reach, pieces=(), held_as=jnp.bfloat16):
    entries = jax.random.normal(key, shape, jnp.float32) * scale
    if len(pieces) > 0:
        entries = level_of(key, shape, pieces, -0.22, 0.18) * entries
    return jnp.clip(entries, min=-reach, max=reach).astype(held_as)


def bell_draw_with(rng, dims, scale, limit, cuts, heavy, held_as=jnp.bfloat16):
    entries = scale * jax.random.normal(rng, dims, jnp.float32)
    if cuts:
        entries = entries * level_of(rng, dims, cuts, -0.22, 0.18)
    return jnp.clip(strengthened(entries, jax.random.fold_in(rng, 3), *heavy), -limit, limit).astype(held_as)


def setup_inputs(seed: int = 0) -> dict:
    streams_of = jax.random.split(jax.random.key(seed), 6)
    return {
        "grads": bell_draw_with(streams_of[0], (MATS, GROUPS, D, D), 0.0625, 0.5, ((1, 32), (2, 8)), (1, 3, 32, 2.75)),
        "basis": centred(streams_of[1], (MATS, D, RANK), RANK ** -0.5, 0.375, ((1, 8),), jnp.float32),
        "weight": centred(streams_of[2], (MATS, N_SHARD, N_DP, ROWW, D), 1.0, 6.0, ((1, 8), (2, 32)), jnp.float32),
        "moment_m": centred(streams_of[3], (MATS, D, RANK), 1.0, 6.0, ((1, 32),), jnp.float32),
        "moment_v": jnp.clip(jnp.exp(math.log(4.0) - 2.7725887 * jax.random.uniform(streams_of[4], (MATS, D, RANK), jnp.float32) ** level_of(streams_of[4], (MATS, D, RANK), ((1, 32),), -0.2, 0.2)), 0.25, 4.0),
    }


def adam_step(moment_m, moment_v, projected):
    next_m = 0.9 * moment_m + 0.1 * projected
    next_v = 0.999 * moment_v + 0.001 * projected * projected
    update = 2.0 * (next_m / (1.0 - 0.9 ** 10)) / (jnp.sqrt(next_v / (1.0 - 0.999 ** 10)) + 1e-08)
    return (next_m, next_v, update)

def newton_schulz(iterate):
    for step in range(NS_STEPS):
        gram = jnp.dot(iterate.T, iterate, precision=lax.Precision.HIGHEST)
        iterate = 1.5 * iterate - 0.5 * jnp.dot(iterate, gram, precision=lax.Precision.HIGHEST)
    return iterate

def reference(grads, basis, weight, moment_m, moment_v):
    weights_out, firsts, seconds, bases = ([], [], [], [])
    for matrix in range(MATS):
        basis_bf = basis[matrix].astype(jnp.bfloat16)
        projected = jnp.zeros((D, RANK), jnp.float32)
        for group in range(GROUPS):
            projected = projected + lax.dot_general(grads[matrix, group], basis_bf, (((0,), (0,)), ((), ())), preferred_element_type=jnp.float32)
        next_m, next_v, update = adam_step(moment_m[matrix], moment_v[matrix], projected)
        delta = jnp.dot(basis[matrix], update.T, precision=lax.Precision.HIGHEST)
        flat_weight = weight[matrix].reshape(D, D)
        weights_out.append((flat_weight - delta).reshape(weight.shape[1:]))
        projected_bf = projected.astype(jnp.bfloat16)
        refresh = jnp.zeros((D, RANK), jnp.float32)
        for group in range(GROUPS):
            refresh = refresh + jnp.dot(grads[matrix, group], projected_bf, preferred_element_type=jnp.float32)
        iterate = refresh / jnp.sqrt(jnp.sum(refresh * refresh) + 1e-06)
        bases.append(newton_schulz(iterate))
        firsts.append(next_m)
        seconds.append(next_v)
    return (jnp.stack(weights_out), jnp.stack(firsts), jnp.stack(seconds), jnp.stack(bases))
```

```python
import jax
import jax.numpy as jnp
from jax import lax
from jax.experimental import pallas as pl
from jax.experimental.pallas import tpu as pltpu
from jax.sharding import PartitionSpec as P

MESH = pl.DeviceIdType.MESH
NX, NY, NZ = 4, 4, 8
NS_STEPS = 5
F32, BF16 = jnp.float32, jnp.bfloat16
N_SEMS = 160

NN = (((1,), (0,)), ((), ()))
NT = (((1,), (1,)), ((), ()))
TN = (((0,), (0,)), ((), ()))


def split(a):
    hi = a.astype(BF16)
    return hi, (a - hi.astype(F32)).astype(BF16)


def dot3(a, b, dims=NN):
    ah, al = a
    bh, bl = b

    def d(p, q):
        return lax.dot_general(p, q, dims, preferred_element_type=F32)

    return d(ah, bh) + (d(ah, bl) + d(al, bh))


def kernel(
    grads, basis, weight, mom_m, mom_v,
    w_out, m_out, v_out, b_out,
    gbuf, bas, wbuf, mbuf, vbuf, mo, vo,
    pf, pbf, r1, acc, r2, p2, r3, pblk, pfull,
    rpart, q1, qacc, q2, rfull, spart, s3, sfull,
    dlt, d1, d2, d3, xbuf,
    lsem, ssem, rsem,
):
    dp = lax.axis_index("dp")
    z = lax.axis_index("shard")
    c = lax.rem(dp, 2)
    chip = lax.div(dp, 2)
    x = lax.rem(chip, NX)
    y = lax.div(chip, NX)
    other = 1 - c

    def at(yy, xx, cc, zz):
        return ((yy * NX + xx) * 2 + cc, zz)

    partner = at(y, x, other, z)
    xs = [lax.rem(x + d, NX) for d in range(NX)]
    ys = [lax.rem(y + d, NY) for d in range(NY)]
    zs = [lax.rem(z + d, NZ) for d in range(NZ)]
    xdev = [at(y, xs[d], c, z) for d in range(NX)]
    ydev = [at(ys[d], x, c, z) for d in range(NY)]
    zdev = [at(y, x, c, zs[d]) for d in range(NZ)]

    used = [0]

    def take(n=1):
        base = used[0]
        used[0] += n
        return base

    def rcopy(src, dst, device, index):
        return pltpu.make_async_remote_copy(
            src_ref=src, dst_ref=dst, send_sem=ssem.at[index], recv_sem=rsem.at[index],
            device_id=device, device_id_type=MESH,
        )

    pending = []

    def send(src, dst, device):
        copy = rcopy(src, dst, device, take())
        copy.start()
        pending.append(copy)
        return copy

    def recv(copies):
        for copy in copies:
            copy.wait_recv()

    local = [0]

    def load(src, dst):
        copy = pltpu.make_async_copy(src, dst, lsem.at[local[0]])
        local[0] += 1
        copy.start()
        return copy

    l_grad = load(grads.at[c, 0], gbuf.at[0])
    l_bas = load(basis.at[c], bas)
    l_m = load(mom_m.at[c], mbuf.at[c])
    l_v = load(mom_v.at[c], vbuf.at[c])
    l_w = load(weight.at[:, 0, 0], wbuf)

    barrier = pltpu.get_barrier_semaphore()
    peers = [partner] + xdev[1:] + ydev[1:] + zdev[1:]
    for peer in peers:
        pl.semaphore_signal(barrier, inc=1, device_id=peer, device_id_type=MESH)
    pl.semaphore_wait(barrier, len(peers))

    order = [1, 2, 3, 0]
    g_copies = {}
    for dy in order:
        cols = pl.ds(pl.multiple_of(ys[dy] * 1024, 1024), 1024)
        g_copies[dy] = send(grads.at[other, 0, :, cols], gbuf.at[1, :, cols], partner)
    m_copy = send(mom_m.at[other], mbuf.at[c], partner)
    v_copy = send(mom_v.at[other], vbuf.at[c], partner)

    l_bas.wait()
    bas_bf = bas[...].astype(BF16)
    l_grad.wait()

    def block_of(i, yy, xx):
        cols = pl.ds(pl.multiple_of((yy * NX + xx) * 256, 256), 256)
        return lax.dot_general(
            gbuf[i, :, cols], bas_bf, TN, preferred_element_type=F32
        ).reshape(2, 128, 256)

    @pl.loop(0, NX * NY)
    def _(b):
        yy, xx = lax.div(b, NX), lax.rem(b, NX)
        pf[yy, xx] = block_of(0, yy, xx)

    s0 = take(12)
    s1 = take(12)

    def first0(dy, dx):
        xx = lax.rem(x + dx, NX)
        return rcopy(
            pbf.at[ys[dy], xx, 0], r1.at[0, dx - 1, ys[dy]], at(y, xx, c, z), s0 + dy * 3 + dx - 1
        )

    def first1(dy, dx):
        xx = lax.rem(x + dx, NX)
        return rcopy(
            pbf.at[ys[dy], xx, 1], r1.at[1, dy - 1, xx], ydev[dy], s1 + (dy - 1) * 4 + dx
        )

    for dy in order:
        g_copies[dy].wait_recv()

        @pl.loop(1, NX + 1)
        def _(step):
            dx = lax.rem(step, NX)
            xx = lax.rem(x + dx, NX)
            yy = ys[dy]
            value = pf[yy, xx] + block_of(1, yy, xx)
            pf[yy, xx] = value
            pbf[yy, xx] = value.astype(BF16)

            @pl.when(step < NX)
            def _():
                first0(dy, dx).start()

            if dy:
                first1(dy, dx).start()

    second0, second1 = {}, {}
    for d in order:
        for e in range(1, NX):
            first0(d, e).wait_recv()
        total = pf[ys[d], x, 0]
        for e in range(NX - 1):
            total += r1[0, e, ys[d]].astype(F32)
        acc[0, d] = total
        if d:
            second0[d] = send(acc.at[0, d], r2.at[0, d - 1], ydev[d])
        for e in range(1, NY):
            first1(e, d).wait_recv()
        total = pf[y, xs[d], 1]
        for e in range(NY - 1):
            total += r1[1, e, xs[d]].astype(F32)
        acc[1, d] = total
        if d:
            second1[d] = send(acc.at[1, d], r2.at[1, d - 1], xdev[d])

    third = {}
    for h, copies in ((0, second0), (1, second1)):
        recv(copies.values())
        p2[h] = (acc[h, 0] + r2[h, 0] + (r2[h, 1] + r2[h, 2])).reshape(4, 32, 256)
    p2v = p2
    for d in range(1, NZ):
        zz = zs[d]
        third[d] = send(p2v.at[lax.div(zz, 4), lax.rem(zz, 4)], r3.at[d - 1], zdev[d])
    recv(third.values())
    zh, zl = lax.div(z, 4), lax.rem(z, 4)
    total = p2v[zh, zl]
    for d in range(1, NZ):
        total += r3[d - 1]
    pblk[z] = total
    pfull[y, x, zh, zl] = total.astype(BF16)

    z_bf = [send(pfull.at[y, x, zh, zl], pfull.at[y, x, zh, zl], zdev[d]) for d in range(1, NZ)]
    z_f = [send(pblk.at[z], pblk.at[z], zdev[d]) for d in range(1, NZ)]
    recv(z_bf)

    def gather_first(full):
        a = [send(full.at[y, x, 0], full.at[y, x, 0], ydev[d]) for d in range(1, NY)]
        b = [send(full.at[y, x, 1], full.at[y, x, 1], xdev[d]) for d in range(1, NX)]
        return a + b

    def gather_second(full):
        a = [send(full.at[:, x, 0], full.at[:, x, 0], xdev[d]) for d in range(1, NX)]
        b = [send(full.at[y, :, 1], full.at[y, :, 1], ydev[d]) for d in range(1, NY)]
        return a + b

    copies = gather_first(pfull)

    recv(z_f)
    l_m.wait()
    l_v.wait()
    m_copy.wait_recv()
    v_copy.wait_recv()
    proj = pblk[...].reshape(256, 256)
    next_m = 0.9 * mbuf[...].reshape(256, 256) + 0.1 * proj
    next_v = 0.999 * vbuf[...].reshape(256, 256) + 0.001 * proj * proj
    mo[...] = next_m.reshape(2, 128, 256)
    vo[...] = next_v.reshape(2, 128, 256)
    update = 2.0 * (next_m / (1.0 - 0.9**10)) / (jnp.sqrt(next_v / (1.0 - 0.999**10)) + 1e-08)

    recv(copies)
    copies = gather_second(pfull)
    out_local = [load(mo.at[c], m_out.at[c]), load(vo.at[c], v_out.at[c])]
    out_remote = [send(mo.at[other], m_out.at[c], partner), send(vo.at[other], v_out.at[c], partner)]
    up = split(update)
    for i in range(4):
        rows = pl.ds(i * 128, 128)
        dlt[i] = dot3(split(bas[rows]), up, NT).reshape(4, 2, 16, 256)
    d1[x] = dlt[:, x].reshape(4, 2, 16, 256)
    recv(copies)

    x_copies = [send(dlt.at[:, xs[d]], d1.at[x], xdev[d]) for d in range(1, NX)]

    for yy in range(NY):
        cols = pl.ds(yy * 1024, 1024)
        right = pfull[yy].reshape(1024, 256)
        for i in range(2):
            part = jnp.dot(gbuf[i, :, cols], right, preferred_element_type=F32)
            part = part.reshape(4, 4, 2, 16, 256)
            if yy == 0 and i == 0:
                rpart[...] = part
            else:
                rpart[...] += part

    def reduce_first():
        a = {d: send(rpart.at[:, xs[d], 0], q1.at[0, d - 1], xdev[d]) for d in range(1, NX)}
        b = {d: send(rpart.at[ys[d], :, 1], q1.at[1, d - 1], ydev[d]) for d in range(1, NY)}
        return a, b

    a, b = reduce_first()
    recv(x_copies)
    d2[y] = d1[:, y]
    recv(a.values())
    qacc[0] = rpart[:, x, 0] + q1[0, 0] + (q1[0, 1] + q1[0, 2])
    a2 = [send(qacc.at[0, ys[d]], q2.at[0, d - 1], ydev[d]) for d in range(1, NY)]
    recv(b.values())
    qacc[1] = rpart[y, :, 1] + q1[1, 0] + (q1[1, 1] + q1[1, 2])
    b2 = [send(qacc.at[1, xs[d]], q2.at[1, d - 1], xdev[d]) for d in range(1, NX)]
    y_copies = [send(d1.at[:, ys[d]], d2.at[y], ydev[d]) for d in range(1, NY)]
    recv(a2)
    rfull[y, x, 0] = qacc[0, y] + q2[0, 0] + (q2[0, 1] + q2[0, 2])
    recv(b2)
    rfull[y, x, 1] = qacc[1, x] + q2[1, 0] + (q2[1, 1] + q2[1, 2])
    copies = gather_first(rfull)
    recv(copies)
    copies = gather_second(rfull)
    recv(y_copies)
    w_copy = send(d2.at[:, :, other], d3, partner)
    recv(copies)

    rsplit = split(rfull[...].reshape(512, 256))
    spart[...] = dot3(rsplit, rsplit, TN).reshape(4, 4, 2, 8, 256)
    s_copies = [send(spart.at[y, x], s3.at[d - 1], zdev[d]) for d in range(1, NZ)]

    l_w.wait()
    w_copy.wait_recv()
    for b16 in range(16):
        yy, xx = b16 // 4, b16 % 4
        cols = pl.ds(b16 * 256, 256)
        wbuf[c, :, cols] = wbuf[c, :, cols] - d2[yy, xx, c]
        wbuf[other, :, cols] = wbuf[other, :, cols] - d3[yy, xx]
    out_local.append(load(wbuf, w_out.at[:, 0, 0]))

    recv(s_copies)
    total = spart[y, x]
    for d in range(1, NZ):
        total += s3[d - 1]
    sfull[y, x] = total
    copies = gather_first(sfull)
    recv(copies)
    copies = gather_second(sfull)
    recv(copies)

    gram = sfull[...].reshape(256, 256)
    eye = lax.broadcasted_iota(jnp.int32, (256, 256), 0) == lax.broadcasted_iota(jnp.int32, (256, 256), 1)
    total_sq = jnp.sum(jnp.where(eye, gram, 0.0), keepdims=True) + 1e-06
    gram = gram / total_sq
    diag = jnp.where(eye, 1.5, 0.0)
    factor = diag - 0.5 * gram
    poly = factor
    for _ in range(1, NS_STEPS):
        fs = split(factor)
        gram = dot3(split(dot3(split(gram), fs)), fs)
        factor = diag - 0.5 * gram
        poly = dot3(split(poly), split(factor))
    poly = split(poly * lax.rsqrt(total_sq))
    xbuf[...] = dot3(split(rfull[...].reshape(512, 256)), poly)
    out_local.append(load(xbuf, b_out.at[c]))
    out_remote.append(send(xbuf, b_out.at[c], partner))

    recv(out_remote)
    for copy in out_local:
        copy.wait()
    for copy in pending:
        copy.wait_send()
    for dy in range(NY):
        for dx in range(NX):
            if dx:
                first0(dy, dx).wait_send()
            if dy:
                first1(dy, dx).wait_send()


def shards(grads, basis, weight, moment_m, moment_v):
    hbm = pl.BlockSpec(memory_space=pl.ANY)
    V = pltpu.VMEM
    return tuple(
        pl.pallas_call(
            kernel,
            out_shape=(
                jax.ShapeDtypeStruct(weight.shape, F32),
                jax.ShapeDtypeStruct(moment_m.shape, F32),
                jax.ShapeDtypeStruct(moment_v.shape, F32),
                jax.ShapeDtypeStruct(basis.shape, F32),
            ),
            in_specs=[hbm] * 5,
            out_specs=(hbm,) * 4,
            scratch_shapes=[
                V((2, 512, 4096), BF16),
                V((512, 256), F32),
                V((2, 16, 4096), F32),
                V((2, 128, 256), F32),
                V((2, 128, 256), F32),
                V((2, 128, 256), F32),
                V((2, 128, 256), F32),
                V((4, 4, 2, 128, 256), F32),
                V((4, 4, 2, 128, 256), BF16),
                V((2, 3, 4, 128, 256), BF16),
                V((2, 4, 128, 256), F32),
                V((2, 3, 128, 256), F32),
                V((2, 4, 32, 256), F32),
                V((7, 32, 256), F32),
                V((8, 32, 256), F32),
                V((4, 4, 2, 4, 32, 256), BF16),
                V((4, 4, 2, 16, 256), F32),
                V((2, 3, 4, 16, 256), F32),
                V((2, 4, 16, 256), F32),
                V((2, 3, 16, 256), F32),
                V((4, 4, 2, 16, 256), F32),
                V((4, 4, 2, 8, 256), F32),
                V((7, 2, 8, 256), F32),
                V((4, 4, 2, 8, 256), F32),
                V((4, 4, 2, 16, 256), F32),
                V((4, 4, 2, 16, 256), F32),
                V((4, 4, 2, 16, 256), F32),
                V((4, 4, 16, 256), F32),
                V((512, 256), F32),
                pltpu.SemaphoreType.DMA((12,)),
                pltpu.SemaphoreType.DMA((N_SEMS,)),
                pltpu.SemaphoreType.DMA((N_SEMS,)),
            ],
            compiler_params=pltpu.CompilerParams(
                collective_id=0, has_side_effects=True, vmem_limit_bytes=60 * 1024 * 1024
            ),
        )(grads, basis, weight, moment_m, moment_v)
    )


def solution(mesh):
    placed = (
        P(None, "dp", "shard", None),
        P(None, "shard", None),
        P(None, "shard", "dp", None, None),
        P(None, "dp", None),
        P(None, "dp", None),
    )
    return jax.shard_map(
        shards,
        mesh=mesh,
        in_specs=placed,
        out_specs=(
            P(None, "shard", "dp", None, None),
            P(None, "dp", None),
            P(None, "dp", None),
            P(None, "shard", None),
        ),
        check_vma=False,
    )
```
